32 devices in a mesh: row: 8 (over z, y), col: 4 (over x, core).
Axes of the slice: x: 2, y: 2, z: 4, core: 2. Of those that a mesh axis runs over, the one named last changes fastest.
Arguments:
- tokens: bfloat16 [4096, 2048], P(('row', 'col')), may hold values from -6 to 6
- seq_lengths: int32 [8, 6], P('row'), may hold values from 1 to 256, 512 in all within a row
- routed_expert_index: int32 [4096, 6], P(('row', 'col')), may hold values from 0 to 63, all different within a row; in each aligned block of 128 rows (0 to 127, 128 to 255, ...) at most 18 rows name the same one
- routed_gate_weight: float32 [4096, 6], P(('row', 'col')), may hold values from 0.05 to 0.5
- gain_attn: bfloat16 [2048], P(('row', 'col')), may hold values from 0.5 to 1.5
- w_query: bfloat16 [2048, 3072], P('row', 'col'), may hold values from -3 to 3
- w_latent: bfloat16 [2048, 576], P(('row', 'col')), may hold values from -0.125 to 0.125
- gain_latent: bfloat16 [512], P(('row', 'col')), may hold values from 0.5 to 1.5
- w_kv_up: bfloat16 [512, 4096], P('row', 'col'), may hold values from -0.25 to 0.25
- w_out: bfloat16 [2048, 2048], P('col', 'row'), may hold values from -0.5 to 0.5
- gain_ffn: bfloat16 [2048], P(('row', 'col')), may hold values from 0.5 to 1.5
- w_shared_gate: bfloat16 [2048, 2816], P('row', 'col'), may hold values from -0.125 to 0.125
- w_shared_up: bfloat16 [2048, 2816], P('row', 'col'), may hold values from -0.125 to 0.125
- w_shared_down: bfloat16 [2816, 2048], P('col', 'row'), may hold values from -0.109375 to 0.109375
- expert_gate_weight: bfloat16 [128, 704, 2048], P(('row', 'col')), may hold values from -0.125 to 0.125
- expert_up_weight: bfloat16 [128, 704, 2048], P(('row', 'col')), may hold values from -0.125 to 0.125
- expert_down_weight: bfloat16 [128, 704, 2048], P(('row', 'col')), may hold values from -0.3125 to 0.3125
- cotangent: bfloat16 [4096, 2048], P(('row', 'col')), may hold values from -6 to 6
Outputs:
- layer_output: bfloat16 [4096, 2048], P(('row', 'col'))
- input_gradient: bfloat16 [4096, 2048], P(('row', 'col'))
- grad_gain_attn: float32 [2048], P(('row', 'col'))
- grad_w_query: float32 [2048, 3072], P('row', 'col')
- grad_w_latent: float32 [2048, 576], P(('row', 'col'))
- grad_gain_latent: float32 [512], P(('row', 'col'))
- grad_w_kv_up: float32 [512, 4096], P('row', 'col')
- grad_w_out: float32 [2048, 2048], P('col', 'row')
- grad_gain_ffn: float32 [2048], P(('row', 'col'))
- grad_shared_gate: float32 [2048, 2816], P('row', 'col')
- grad_shared_up: float32 [2048, 2816], P('row', 'col')
- grad_shared_down: float32 [2816, 2048], P('col', 'row')
- grad_expert_gate: float32 [128, 704, 2048], P(('row', 'col'))
- grad_expert_up: float32 [128, 704, 2048], P(('row', 'col'))
- grad_expert_down: float32 [128, 704, 2048], P(('row', 'col'))
The draws below stay inside these ranges and needn't reach their ends.
Inputs may be any that keep to these rules, and one draw needn't show every extreme that they name: Each token's row of routed_expert_index names 6 different experts; among the 128 tokens of one device no expert is named more than 18 times, and that many is reached. `seq_lengths`: each group's lengths sum to 512, the longest being 256.
All inputs are finite; a program needn't handle non-finite values.
Results may differ from the reference program's by a relative error of at most 0.025.
The reference program's roundings to bfloat16 on the way count: a program that leaves them out, or rounds other values in their place, can miss the bound.
Values may be sent and summed in bfloat16 or wider, within the bound.
No kernel may reach another device: no remote copies, remote signals or barrier semaphores. Data moves between devices by JAX's collectives and lax.ppermute only.
A program may use at most 448 MiB of HBM per device.

```python
import math
import jax
import jax.numpy as jnp
import numpy as np
from jax import lax

D = 2048
H = 16
DN = 128
DR = 64
DV = 128
DC = 512
E = 64
FFE = 1408
TOPK = 6
TOK_DEV = 128
SEQS = 6
FFS = 2816
FFH = 704
GROUP_TOK = 512
GROUPS = 8
TOKENS = 4096
MAXLEN = 256
CAP = 18
N_ROW = 8
N_COL = 4


def draw_w_query(key, part):
    width = DN + DR
    base = jax.random.normal(key, (D, H, width), jnp.float32) * D ** (-0.5)
    return jnp.clip(base, -3.0, 3.0).reshape(D, H * width).astype(jnp.bfloat16)


def levels(own_key, dims, pieces, smallest, top_value):
    def one(dim, blocks):
        steps = jax.random.uniform(jax.random.fold_in(jax.random.fold_in(own_key, 6), dim), (blocks,), jnp.float32, smallest / len(pieces), top_value / len(pieces))
        return jnp.repeat(jnp.exp(steps), dims[dim] // blocks).reshape((-1,) + (1,) * (len(dims) - dim - 1))

    loudness = one(*pieces[0])
    for cut in pieces[1:]:
        loudness = loudness * one(*cut)
    return loudness


def split_up(count, total, bound, skew):
    loads = [(1 << 20) // math.isqrt(grade ** skew) + 1 for grade in range(2, count + 1)]
    surplus, given = total - bound - (count - 1), [1] * (count - 1)
    while surplus > 0:
        free = [i for i in range(count - 1) if given[i] < bound]
        whole, remaining = sum([loads[i] for i in free]), surplus
        for i in free:
            more = min(bound - given[i], max(1, remaining * loads[i] // whole), surplus)
            given[i] = given[i] + more
            surplus = surplus - more
    return np.array([bound] + given)


def uneven(rng, number_of, total, limit, skew):
    if number_of == 2:
        one = jax.random.randint(rng, (), max(1, total - limit), min(limit, total - 1) + 1)
        return jnp.stack([one, total - one])
    sizes = jnp.asarray(split_up(number_of, total, limit, skew), jnp.int32)
    pairs = (number_of - 1) // 2
    donor, sink = sizes[1:1 + 2 * pairs:2], sizes[2:2 + 2 * pairs:2]
    slack = jnp.minimum(donor - 1, limit - sink)
    passed = jax.random.randint(jax.random.fold_in(rng, 1), (pairs,), 0, 1 << 20) % (slack + 1)
    sizes = sizes.at[1:1 + 2 * pairs:2].set(donor - passed).at[2:2 + 2 * pairs:2].set(sink + passed)
    return sizes[jax.random.permutation(jax.random.fold_in(rng, 2), number_of)]


def routed_block(stream_key, own, number, rows, number_of, top, reach, skew):
    ranking = jax.random.permutation(stream_key, number_of)
    packed, ordinary = load_shares(number_of, rows * top, reach, skew, True), load_shares(number_of, rows * top, reach, skew, False)
    places = jnp.arange(number_of)

    def named(sizes, offset_by):
        used = int((sizes > 0).sum())
        fixed = max(1, used // 4)
        moved = fixed + (places - fixed + offset_by * (used - fixed)) % max(1, number_of - fixed)
        return jnp.zeros((number_of,), jnp.int32).at[ranking[jnp.where(places < fixed, places, moved)]].set(jnp.asarray(sizes, jnp.int32))

    sizes = jnp.where(number % 4 == 0, named(packed, number // 4), named(ordinary, number - number // 4 - 1))
    mixed = jax.random.permutation(jax.random.fold_in(own, 3), number_of)
    source_of, receiver = mixed[0:number_of // 2 * 2:2], mixed[1:number_of // 2 * 2:2]
    slack = jnp.minimum(sizes[source_of] - 1, reach - sizes[receiver]) // 2
    slack = jnp.where((source_of == ranking[0]) | (receiver == ranking[0]) | (sizes[receiver] == 0), 0, jnp.maximum(slack, 0))
    moved = jax.random.randint(jax.random.fold_in(own, 4), (number_of // 2,), 0, 1 << 20) % (slack + 1)
    sizes = sizes.at[source_of].add(-moved).at[receiver].add(moved)
    items = jnp.searchsorted(jnp.cumsum(sizes), jnp.arange(rows * top), side="right").astype(jnp.int32)
    listing = items.reshape(top, rows).T
    listing = listing[jax.random.permutation(jax.random.fold_in(own, 1), rows)]
    offset_by = jax.random.randint(jax.random.fold_in(own, 2), (rows, 1), 0, top)
    return jnp.take_along_axis(listing, (jnp.arange(top)[None, :] + offset_by) % top, axis=1)


def load_shares(number_of, total, most, lean, full):
    loads = [(1 << 20) // math.isqrt(grade ** lean) + 1 for grade in range(1, number_of + 1)]
    largest = most if full else min(most, max(-(-total // number_of), total * loads[0] // sum(loads)))
    least = 1 if total - largest >= number_of - 1 else 0
    holding, surplus = [largest] + [least] * (number_of - 1), total - largest - least * (number_of - 1)
    while surplus > 0:
        movable = [i for i in range(1, number_of) if holding[i] < largest] or [i for i in range(1, number_of) if holding[i] < most]
        whole, left = sum([loads[i] for i in movable]), surplus
        for i in movable:
            more = min(most - holding[i], max(1, left * loads[i] // whole), surplus)
            holding[i] = holding[i] + more
            surplus = surplus - more
    return np.array(holding)


def centred(rng, extent, spread, limit, pieces=(), kind=jnp.bfloat16):
    loudness = levels(rng, extent, pieces, -0.22, 0.18) if pieces else 1.0
    array = jax.random.normal(rng, extent, jnp.float32) * spread * loudness
    return jnp.minimum(jnp.maximum(array, -limit), limit).astype(kind)


def setup_inputs(seed: int = 0) -> dict:
    arg_keys = jax.random.split(jax.random.key(seed), 19)
    tokens = centred(arg_keys[0], (TOKENS, D), 1.0, 6.0, ((0, 32),))
    seq_lengths = jax.vmap(lambda own: uneven(own, SEQS, GROUP_TOK, MAXLEN, 2))(jax.random.split(arg_keys[1], GROUPS)).reshape((GROUPS, SEQS)).astype(jnp.int32)
    routed_expert_index_keys = jax.random.split(jax.random.fold_in(arg_keys[2], 1), TOKENS // TOK_DEV)
    routed_expert_index_turns = jax.random.permutation(jax.random.fold_in(arg_keys[2], 3), TOKENS // TOK_DEV)
    routed_expert_index = jax.vmap(lambda own, number: routed_block(jax.random.fold_in(arg_keys[2], 2), own, number, TOK_DEV, E, TOPK, CAP, 2))(routed_expert_index_keys, routed_expert_index_turns).reshape((TOKENS, TOPK))
    routed_gate_weight = jnp.clip(0.05 + 0.45 * jax.random.uniform(arg_keys[3], (TOKENS, TOPK), jnp.float32) ** levels(arg_keys[3], (TOKENS, TOPK), ((0, 32),), -0.2, 0.2), 0.05, 0.5)
    gain_attn = jnp.clip(1.0 + 0.1 * jax.random.normal(arg_keys[4], (D,), jnp.float32), 0.5, 1.5).astype(jnp.bfloat16)
    w_query = draw_w_query(jax.random.fold_in(arg_keys[18], 71), 0)
    w_latent = centred(arg_keys[6], (D, DC + DR), D ** -0.5, 0.125, ((0, 32),))
    gain_latent = jnp.clip(1.0 + 0.1 * jax.random.normal(arg_keys[7], (DC,), jnp.float32), 0.5, 1.5).astype(jnp.bfloat16)
    w_kv_up = centred(arg_keys[8], (DC, H * (DN + DV)), DC ** -0.5, 0.25, ((0, 8), (1, 4)))
    w_out = centred(arg_keys[9], (H * DV, D), (H * DV // 16) ** -0.5, 0.5, ((0, 4), (1, 8)))
    gain_ffn = jnp.clip(1.0 + 0.1 * jax.random.normal(arg_keys[10], (D,), jnp.float32), 0.5, 1.5).astype(jnp.bfloat16)
    w_shared_gate = centred(arg_keys[11], (D, FFS), D ** -0.5, 0.125, ((0, 8), (1, 4)))
    w_shared_up = centred(arg_keys[12], (D, FFS), D ** -0.5, 0.125, ((0, 8), (1, 4)))
    w_shared_down = centred(arg_keys[13], (FFS, D), FFS ** -0.5, 0.109375, ((0, 4), (1, 8)))
    expert_gate_weight = centred(arg_keys[14], (2 * E, FFH, D), D ** -0.5, 0.125, ((0, 32),))
    expert_up_weight = centred(arg_keys[15], (2 * E, FFH, D), D ** -0.5, 0.125, ((0, 32),))
    expert_down_weight = centred(arg_keys[16], (2 * E, FFH, D), (FFE // 4) ** -0.5, 0.3125, ((0, 32),))
    cotangent = centred(arg_keys[17], (TOKENS, D), 1.0, 6.0, ((0, 32),))
    return dict(tokens=tokens, seq_lengths=seq_lengths, routed_expert_index=routed_expert_index, routed_gate_weight=routed_gate_weight, gain_attn=gain_attn, w_query=w_query, w_latent=w_latent, gain_latent=gain_latent, w_kv_up=w_kv_up, w_out=w_out, gain_ffn=gain_ffn, w_shared_gate=w_shared_gate, w_shared_up=w_shared_up, w_shared_down=w_shared_down, expert_gate_weight=expert_gate_weight, expert_up_weight=expert_up_weight, expert_down_weight=expert_down_weight, cotangent=cotangent)


EPS = 1e-06
NEG = -1e+30

def widen(values):
    return lax.optimization_barrier(values).astype(jnp.float32)

def inv_rms(rows):
    return lax.rsqrt(lax.optimization_barrier(jnp.mean(rows * rows, axis=-1, keepdims=True)) + EPS)

def norm_gradient_pass(grad_out, normed, factor, gain):
    scaled = grad_out * gain
    return factor * (scaled - normed * lax.optimization_barrier(jnp.mean(scaled * normed, axis=-1, keepdims=True)))

def swish_parts(pre):
    sig = jax.nn.sigmoid(pre)
    return (pre * sig, sig * (1.0 + pre * (1.0 - sig)))

def rope_tables(position, width):
    half = width // 2
    freq = jnp.exp(jnp.arange(half, dtype=jnp.float32) * (-2.0 * math.log(10000.0) / width))
    angle = position.astype(jnp.float32)[:, None] * freq[None, :]
    return (jnp.cos(angle), jnp.sin(angle))

def rotate(values, cosine, sine):
    half = values.shape[-1] // 2
    first, second = (values[..., :half], values[..., half:])
    return jnp.concatenate([first * cosine - second * sine, first * sine + second * cosine], axis=-1)

def unrotate(grads, cosine, sine):
    half = grads.shape[-1] // 2
    first, second = (grads[..., :half], grads[..., half:])
    return jnp.concatenate([first * cosine + second * sine, second * cosine - first * sine], axis=-1)

def seq_layout(lengths, count):
    ends = jnp.cumsum(lengths).astype(jnp.int32)
    where = jnp.arange(count, dtype=jnp.int32)
    after = where[:, None] >= ends[None, :]
    segment = lax.optimization_barrier(jnp.sum(after.astype(jnp.int32), axis=1)).astype(jnp.int32)
    begin = lax.optimization_barrier(jnp.sum(jnp.where(after, lengths[None, :], 0), axis=1)).astype(jnp.int32)
    return (segment, where - begin)

def group_forward(normed_input, ckv, lengths, w_query, w_kv_up):
    count = normed_input.shape[0]
    segment, position = seq_layout(lengths, count)
    cosine, sine = rope_tables(position, DR)
    query = jnp.dot(normed_input, w_query, preferred_element_type=jnp.float32).reshape(count, H, DN + DR)
    query = jnp.concatenate([query[..., :DN], rotate(query[..., DN:], cosine[:, None, :], sine[:, None, :])], axis=-1).astype(jnp.bfloat16)
    pairs = jnp.dot(ckv[:, :DC], w_kv_up, preferred_element_type=jnp.float32).astype(jnp.bfloat16).reshape(count, H, DN + DV)
    keys = jnp.concatenate([pairs[..., :DN], jnp.broadcast_to(ckv[:, None, DC:], (count, H, DR))], axis=-1)
    values = pairs[..., DN:]
    where = jnp.arange(count, dtype=jnp.int32)
    mask = (segment[:, None] == segment[None, :]) & (where[None, :] <= where[:, None])
    scale = 1.0 / math.sqrt(DN + DR)
    raw = jnp.einsum('qhd,khd->hqk', widen(query), widen(keys)) * scale
    scores = jnp.where(mask[None], raw, NEG)
    top = lax.optimization_barrier(jnp.max(scores, axis=-1, keepdims=True))
    lse = top + jnp.log(lax.optimization_barrier(jnp.sum(jnp.exp(scores - top), axis=-1, keepdims=True)))
    prob = jnp.where(mask[None], jnp.exp(scores - lse), 0.0).astype(jnp.bfloat16)
    out = jnp.einsum('hqk,khd->qhd', widen(prob), widen(values)).astype(jnp.bfloat16)
    return (out.reshape(count, H * DV), (query, keys, values, mask, cosine, sine, scores, lse))

def group_backward(normed_input, ckv, lengths, grad_out, w_query, w_kv_up):
    count = normed_input.shape[0]
    out, saved = group_forward(normed_input, ckv, lengths, w_query, w_kv_up)
    query, keys, values, mask, cosine, sine, scores, lse = saved
    scale = 1.0 / math.sqrt(DN + DR)
    grad_heads = widen(grad_out).reshape(count, H, DV)
    prob = jnp.where(mask[None], jnp.exp(scores - lse), 0.0)
    prob_low = prob.astype(jnp.bfloat16)
    grad_prob = jnp.einsum('qhd,khd->hqk', grad_heads, widen(values))
    delta = lax.optimization_barrier(jnp.sum(prob * grad_prob, axis=-1, keepdims=True))
    grad_score = widen((prob * (grad_prob - delta) * scale).astype(jnp.bfloat16))
    grad_query = jnp.einsum('hqk,khd->qhd', grad_score, widen(keys))
    grad_keys = jnp.einsum('hqk,qhd->khd', grad_score, widen(query))
    grad_values = jnp.einsum('hqk,qhd->khd', widen(prob_low), grad_heads)
    dquery_pre = jnp.concatenate([grad_query[..., :DN], unrotate(grad_query[..., DN:], cosine[:, None, :], sine[:, None, :])], axis=-1)
    dquery_pre = dquery_pre.reshape(count, H * (DN + DR)).astype(jnp.bfloat16)
    dpairs = jnp.concatenate([grad_keys[..., :DN], grad_values], axis=-1).reshape(count, H * (DN + DV)).astype(jnp.bfloat16)
    dkey_rope = lax.optimization_barrier(jnp.sum(grad_keys[..., DN:], axis=1))
    return (dquery_pre, dpairs, dkey_rope)

def expert_halves_joined(second_normed_hidden, output_gradient, routed_expert_index, routed_gate_weight, expert_gate_weight, expert_up_weight, expert_down_weight):
    flat_ids = routed_expert_index.reshape(-1).astype(jnp.int32)
    span = N_ROW * N_COL * CAP
    order = jnp.argsort(flat_ids, stable=True).astype(jnp.int32)
    counts = lax.optimization_barrier(jnp.sum((flat_ids[:, None] == jnp.arange(E, dtype=jnp.int32)[None, :]).astype(jnp.int32), axis=0)).astype(jnp.int32)
    starts = (jnp.cumsum(counts) - counts).astype(jnp.int32)
    order_pad = jnp.concatenate([order, jnp.zeros((span,), jnp.int32)])
    gates_flat = routed_gate_weight.reshape(-1)

    def step(carry, index):
        moe_acc, grad_acc = carry
        picked = lax.dynamic_slice_in_dim(order_pad, starts[index], span)
        live = jnp.arange(span, dtype=jnp.int32) < counts[index]
        rows = (picked // TOPK).astype(jnp.int32)
        inputs = jnp.where(live[:, None], second_normed_hidden[rows].astype(jnp.float32), 0.0)
        weight = jnp.where(live, gates_flat[picked], 0.0)
        dexp = widen((weight[:, None] * output_gradient[rows]).astype(jnp.bfloat16))
        w_gate = lax.dynamic_slice_in_dim(expert_gate_weight, 2 * index, 2).astype(jnp.float32)
        w_up = lax.dynamic_slice_in_dim(expert_up_weight, 2 * index, 2).astype(jnp.float32)
        w_down = lax.dynamic_slice_in_dim(expert_down_weight, 2 * index, 2).astype(jnp.float32)
        pre_gate = jnp.einsum('rd,phd->prh', inputs, w_gate)
        pre_up = jnp.einsum('rd,phd->prh', inputs, w_up)
        act, slope = swish_parts(pre_gate)
        hidden = widen((act * pre_up).astype(jnp.bfloat16))
        halves = widen(jnp.einsum('prh,phd->prd', hidden, w_down).astype(jnp.bfloat16))
        expert_out = widen(lax.optimization_barrier(jnp.sum(halves, axis=0)).astype(jnp.bfloat16))
        moe_acc = moe_acc.at[rows].add(weight[:, None] * expert_out)
        dact = jnp.einsum('rd,phd->prh', dexp, w_down)
        g_down = jnp.einsum('prh,rd->phd', hidden, dexp)
        dgate = widen((dact * pre_up * slope).astype(jnp.bfloat16))
        up_gradient = widen((dact * act).astype(jnp.bfloat16))
        g_gate = jnp.einsum('prh,rd->phd', dgate, inputs)
        g_up = jnp.einsum('prh,rd->phd', up_gradient, inputs)
        dx = jnp.einsum('prh,phd->prd', dgate, w_gate) + jnp.einsum('prh,phd->prd', up_gradient, w_up)
        dx = widen(lax.optimization_barrier(jnp.sum(widen(dx.astype(jnp.bfloat16)), axis=0)).astype(jnp.bfloat16))
        grad_acc = grad_acc.at[rows].add(jnp.where(live[:, None], dx, 0.0))
        return ((moe_acc, grad_acc), (g_gate, g_up, g_down))
    start = (jnp.zeros(second_normed_hidden.shape, jnp.float32), jnp.zeros(second_normed_hidden.shape, jnp.float32))
    (routed_mixture, routed_mixture_gradient), (g_gate, g_up, g_down) = lax.scan(step, start, jnp.arange(E, dtype=jnp.int32))
    shape = (2 * E, FFH, D)
    return (routed_mixture, routed_mixture_gradient, g_gate.reshape(shape), g_up.reshape(shape), g_down.reshape(shape))

def reference(tokens, seq_lengths, routed_expert_index, routed_gate_weight, gain_attn, w_query, w_latent, gain_latent, w_kv_up, w_out, gain_ffn, w_shared_gate, w_shared_up, w_shared_down, expert_gate_weight, expert_up_weight, expert_down_weight, cotangent):
    input_rows = tokens.astype(jnp.float32)
    attention_gradient = gain_attn.astype(jnp.float32)
    g_lat = gain_latent.astype(jnp.float32)
    g_ffn = gain_ffn.astype(jnp.float32)
    first_scale_factor = inv_rms(input_rows)
    normalized_input = input_rows * first_scale_factor
    normed_input = (normalized_input * attention_gradient).astype(jnp.bfloat16)
    segment, position = jax.vmap(seq_layout, in_axes=(0, None))(seq_lengths, GROUP_TOK)
    cosine, sine = rope_tables(position.reshape(-1), DR)
    latent_pre = jnp.dot(normed_input, w_latent, preferred_element_type=jnp.float32)
    pre_lat = latent_pre[:, :DC]
    factor_lat = inv_rms(pre_lat)
    lat_hat = pre_lat * factor_lat
    ckv = jnp.concatenate([(lat_hat * g_lat).astype(jnp.bfloat16), rotate(latent_pre[:, DC:], cosine, sine).astype(jnp.bfloat16)], axis=1)
    x_groups = normed_input.reshape(GROUPS, GROUP_TOK, D)
    c_groups = ckv.reshape(GROUPS, GROUP_TOK, DC + DR)

    def forward_one(args):
        return group_forward(args[0], args[1], args[2], w_query, w_kv_up)[0]
    attended = lax.map(forward_one, (x_groups, c_groups, seq_lengths)).reshape(TOKENS, H * DV)
    hidden = input_rows + jnp.dot(attended, w_out, preferred_element_type=jnp.float32)
    factor_two = inv_rms(hidden)
    hhat = hidden * factor_two
    second_normed_hidden = (hhat * g_ffn).astype(jnp.bfloat16)
    pre_gate = jnp.dot(second_normed_hidden, w_shared_gate, preferred_element_type=jnp.float32)
    pre_up = jnp.dot(second_normed_hidden, w_shared_up, preferred_element_type=jnp.float32)
    act_shared, slope_shared = swish_parts(pre_gate)
    shared_act = (act_shared * pre_up).astype(jnp.bfloat16)
    shared = jnp.dot(shared_act, w_shared_down, preferred_element_type=jnp.float32)
    output_gradient = cotangent.astype(jnp.float32)
    routed_mixture, routed_mixture_gradient, expert_gate_gradient, expert_up_gradient, expert_down_gradient = expert_halves_joined(second_normed_hidden, output_gradient, routed_expert_index, routed_gate_weight, expert_gate_weight, expert_up_weight, expert_down_weight)
    layer_output = (hidden + shared + routed_mixture).astype(jnp.bfloat16)
    dshared = jnp.dot(cotangent, w_shared_down.T, preferred_element_type=jnp.float32)
    common_down_gradient = jnp.dot(shared_act.T, cotangent, preferred_element_type=jnp.float32)
    dgate = (dshared * pre_up * slope_shared).astype(jnp.bfloat16)
    up_gradient = (dshared * act_shared).astype(jnp.bfloat16)
    common_gate_gradient = jnp.dot(second_normed_hidden.T, dgate, preferred_element_type=jnp.float32)
    common_up_gradient = jnp.dot(second_normed_hidden.T, up_gradient, preferred_element_type=jnp.float32)
    dh2n = jnp.dot(dgate, w_shared_gate.T, preferred_element_type=jnp.float32) + jnp.dot(up_gradient, w_shared_up.T, preferred_element_type=jnp.float32) + routed_mixture_gradient
    feedforward_gain_gradient = lax.optimization_barrier(jnp.sum(dh2n * hhat, axis=0))
    hidden_gradient = output_gradient + norm_gradient_pass(dh2n, hhat, factor_two, g_ffn)
    dattn = hidden_gradient.astype(jnp.bfloat16)
    output_weight_gradient = jnp.dot(attended.T, dattn, preferred_element_type=jnp.float32)
    dattended = jnp.dot(dattn, w_out.T, preferred_element_type=jnp.float32).astype(jnp.bfloat16)

    def backward_one(args):
        return group_backward(args[0], args[1], args[2], args[3], w_query, w_kv_up)
    dquery_pre, dpairs, dkey_rope = lax.map(backward_one, (x_groups, c_groups, seq_lengths, dattended.reshape(GROUPS, GROUP_TOK, H * DV)))
    dquery_pre = dquery_pre.reshape(TOKENS, H * (DN + DR))
    dpairs = dpairs.reshape(TOKENS, H * (DN + DV))
    dkey_rope = dkey_rope.reshape(TOKENS, DR)
    query_weight_gradient = jnp.dot(normed_input.T, dquery_pre, preferred_element_type=jnp.float32)
    key_value_gradient = jnp.dot(ckv[:, :DC].T, dpairs, preferred_element_type=jnp.float32)
    dlatent = jnp.dot(dpairs, w_kv_up.T, preferred_element_type=jnp.float32)
    latent_gain_gradient = lax.optimization_barrier(jnp.sum(dlatent * lat_hat, axis=0))
    dlatent_pre = jnp.concatenate([norm_gradient_pass(dlatent, lat_hat, factor_lat, g_lat), unrotate(dkey_rope, cosine, sine)], axis=1).astype(jnp.bfloat16)
    latent_weight_gradient = jnp.dot(normed_input.T, dlatent_pre, preferred_element_type=jnp.float32)
    normed_input_gradient = jnp.dot(dquery_pre, w_query.T, preferred_element_type=jnp.float32) + jnp.dot(dlatent_pre, w_latent.T, preferred_element_type=jnp.float32)
    attention_gain_gradient = lax.optimization_barrier(jnp.sum(normed_input_gradient * normalized_input, axis=0))
    input_gradient = (hidden_gradient + norm_gradient_pass(normed_input_gradient, normalized_input, first_scale_factor, attention_gradient)).astype(jnp.bfloat16)
    return (layer_output, input_gradient, attention_gain_gradient, query_weight_gradient, latent_weight_gradient, latent_gain_gradient, key_value_gradient, output_weight_gradient, feedforward_gain_gradient, common_gate_gradient, common_up_gradient, common_down_gradient, expert_gate_gradient, expert_up_gradient, expert_down_gradient)
```

```python
import math

import jax
import jax.numpy as jnp
from jax import lax
from jax.sharding import PartitionSpec as P

DN = 128
DR = 64
DV = 128
DC = 512
E = 64
CAP = 18


EPS = 1e-06
NEG = -1e30
F32 = jnp.float32
BF16 = jnp.bfloat16


def inv_rms(rows):
    return lax.rsqrt(jnp.mean(rows * rows, axis=-1, keepdims=True) + EPS)


def norm_gradient_pass(grad_out, normed, factor, gain):
    scaled = grad_out * gain
    return factor * (scaled - normed * jnp.mean(scaled * normed, axis=-1, keepdims=True))


def swish_parts(pre):
    sig = jax.nn.sigmoid(pre)
    return (pre * sig, sig * (1.0 + pre * (1.0 - sig)))


def rope_tables(position, width):
    half = width // 2
    freq = jnp.exp(jnp.arange(half, dtype=F32) * (-2.0 * math.log(10000.0) / width))
    angle = freq[:, None] * position.astype(F32)[None, :]
    return (jnp.cos(angle).T, jnp.sin(angle).T)


def rotate(values, cosine, sine):
    half = values.shape[-1] // 2
    first, second = (values[..., :half], values[..., half:])
    return jnp.concatenate(
        [first * cosine - second * sine, first * sine + second * cosine], axis=-1
    )


def unrotate(grads, cosine, sine):
    half = grads.shape[-1] // 2
    first, second = (grads[..., :half], grads[..., half:])
    return jnp.concatenate(
        [first * cosine + second * sine, second * cosine - first * sine], axis=-1
    )


def seq_layout(lengths, where):
    ends = jnp.cumsum(lengths)
    after = where[:, None] >= ends[None, :]
    segment = jnp.sum(after.astype(jnp.int32), axis=1)
    begin = jnp.sum(jnp.where(after, lengths[None, :], 0), axis=1)
    return (segment, where - begin)


def dot(a, b, ca, cb):
    return lax.dot_general(a, b, (((ca,), (cb,)), ((), ())), preferred_element_type=F32)


def col_bits():
    bit, bits = lax.axis_size("col") // 2, []
    while bit:
        bits.append(bit)
        bit //= 2
    return bits


def col_order():
    order = [0]
    for bit in col_bits():
        order = order + [one ^ bit for one in order]
    return order


def col_flip(blocks):
    col = lax.axis_index("col")
    for bit in col_bits():
        on = (col & bit) != 0
        blocks = [jnp.where(on, blocks[k ^ bit], blocks[k]) for k in range(len(blocks))]
    return blocks


def col_swap(block, bit):
    return lax.ppermute(block, "col", [(i, i ^ bit) for i in range(lax.axis_size("col"))])


def col_gather(block):
    for bit in col_bits():
        block = jnp.concatenate([block, col_swap(block, bit)], axis=0)
    return block


def col_scatter(terms):
    for bit in reversed(col_bits()):
        half = terms.shape[0] // 2
        terms = terms[:half] + col_swap(terms[half:].astype(BF16), bit).astype(F32)
    return terms


class Ring:
    def __init__(self):
        n = lax.axis_size("row")
        self.n = n
        ring = list(range(0, n, 2)) + list(range(1, n, 2))[::-1]
        spot = [ring.index(i) for i in range(n)]
        self.ahead = [(ring[i], ring[(i + 1) % n]) for i in range(n)]
        self.behind = [(b, a) for a, b in self.ahead]
        self.most = n // 2
        offsets = [0]
        for step in range(1, self.most + 1):
            offsets.append(-step)
            if step < n - self.most:
                offsets.append(step)
        self.block_of = {off % n: j for j, off in enumerate(offsets)}
        self.ring, self.spot = ring, spot
        self.turns = [off % n for off in offsets]
        index = lax.axis_index("row")
        half = lax.shift_right_logical(index, 1)
        self.me = jnp.where((index & 1) == 0, half, n - 1 - half)

    def gather(self, block):
        a = b = block
        out = [block]
        for step in range(1, self.most + 1):
            a = lax.ppermute(a, "row", self.ahead)
            out.append(a)
            if step < self.n - self.most:
                b = lax.ppermute(b, "row", self.behind)
                out.append(b)
        return out

    def scatter(self, blocks):
        def pick(off):
            return blocks[self.block_of[off % self.n]]

        total = blocks[0]
        if self.n == 1:
            return total
        a = pick(self.most)
        for step in range(self.most - 1, 0, -1):
            a = lax.ppermute(a.astype(BF16), "row", self.ahead).astype(F32) + pick(step)
        total = total + lax.ppermute(a.astype(BF16), "row", self.ahead).astype(F32)
        most = self.n - 1 - self.most
        if most:
            b = pick(-most)
            for step in range(most - 1, 0, -1):
                b = lax.ppermute(b.astype(BF16), "row", self.behind).astype(F32) + pick(-step)
            total = total + lax.ppermute(b.astype(BF16), "row", self.behind).astype(F32)
        return total

    def turn(self, blocks, start, axis):
        size = blocks[0].shape[axis]
        twice = jnp.concatenate(blocks + blocks, axis=axis)
        at = [0] * twice.ndim
        at[axis] = start * size
        shape = list(twice.shape)
        shape[axis] = self.n * size
        turned = lax.dynamic_slice(twice, at, shape, allow_negative_indices=False)
        return self.cut(turned, axis)

    def relative(self, values, axis):
        blocks = self.cut(values, axis)
        blocks = self.turn([blocks[k] for k in self.ring], self.me, axis)
        return [blocks[turn] for turn in self.turns]

    def absolute(self, values, axis):
        blocks = self.cut(values, axis)
        blocks = [blocks[self.block_of[i]] for i in range(self.n)]
        blocks = self.turn(blocks, self.n - self.me, axis)
        return jnp.concatenate([blocks[self.spot[k]] for k in range(self.n)], axis=axis)

    def order_matrix(self, count):
        size = count // self.n
        steps = jnp.arange(count, dtype=jnp.int32)
        turns = jnp.asarray([t for t in self.turns for _ in range(size)], jnp.int32)
        place = self.me + turns
        place = jnp.where(place >= self.n, place - self.n, place)
        owner = jnp.where(2 * place < self.n, 2 * place, 2 * (self.n - 1 - place) + 1)
        wanted = owner * size + steps % size
        return (wanted[None, :] == steps[:, None]).astype(BF16)

    def cut(self, values, axis):
        size = values.shape[axis] // self.n
        return [lax.slice_in_dim(values, j * size, (j + 1) * size, axis=axis) for j in range(self.n)]


def after(value, earlier):
    return value + jnp.where(jnp.isfinite(earlier.astype(F32)), 0.0, 1.0).astype(value.dtype)


class Routes:
    def __init__(self, info, own, topk, cols, rows, per):
        self.joined = per % 2 == 0
        self.units = per // 2 if self.joined else per
        self.cols = cols
        self.places = cols if self.joined else cols // 2
        self.span = rows * CAP
        mine = self.places * self.units
        listed = info.T.astype(F32)
        names = listed[:topk].astype(jnp.int32)
        weights = listed[topk : 2 * topk] + listed[2 * topk : 3 * topk]
        weights = weights + listed[3 * topk : 4 * topk]
        first = lax.axis_index("row") * mine
        experts = first + jnp.arange(mine, dtype=jnp.int32)
        hits = names[None] == experts[:, None, None]
        named = jnp.any(hits, axis=1)
        gates = jnp.sum(jnp.where(hits, weights[None], 0.0), axis=1)
        steps = jnp.arange(own, dtype=jnp.int32)
        earlier = (steps[:, None] < steps[None, :]).astype(BF16)
        before = dot(named.astype(BF16).reshape(mine * rows, own), earlier, 1, 0)
        before = before.astype(jnp.int32).reshape(mine, rows, own)
        before = before + (jnp.arange(rows, dtype=jnp.int32) * CAP)[None, :, None]
        slot = jnp.where(named, before.reshape(mine, rows * own), -1)
        spot = jnp.arange(self.span, dtype=jnp.int32)
        chosen = slot[:, None, :] == spot[None, :, None]
        weighed = jnp.where(chosen, gates[:, None, :], 0.0)
        shape = (mine * self.span, rows * own)
        self.chosen = chosen.astype(BF16).reshape(shape)
        self.gate_of_row = jnp.sum(weighed, axis=2).reshape(shape[0], 1)
        self.gates = weighed.astype(BF16).reshape(shape)

    def send(self, rows):
        width = rows.shape[1]
        parts = rows.reshape(self.places, self.units * self.span, width)
        if not self.joined:
            parts = jnp.broadcast_to(parts[:, None], (self.places, 2) + parts.shape[1:])
            parts = parts.reshape(self.cols, self.units * self.span, width)
        got = lax.all_to_all(parts, "col", split_axis=0, concat_axis=0, tiled=True)
        got = got.reshape(self.cols, self.units, self.span, width)
        return got.transpose(1, 0, 2, 3).reshape(self.units, self.cols * self.span, width)

    def give_back(self, results):
        width = results.shape[-1]
        parts = results.reshape(self.units, self.cols, self.span, width).transpose(1, 0, 2, 3)
        parts = parts.reshape(self.cols, self.units * self.span, width)
        got = lax.all_to_all(parts, "col", split_axis=0, concat_axis=0, tiled=True)
        if not self.joined:
            got = got.reshape((self.places, 2) + got.shape[1:]).astype(F32)
            got = jnp.sum(got, axis=1).astype(BF16)
        return got.reshape(self.places * self.units * self.span, width)


def on_device(
    tokens,
    seq_lengths,
    routed_expert_index,
    routed_gate_weight,
    gain_attn,
    w_query,
    w_latent,
    gain_latent,
    w_kv_up,
    w_out,
    gain_ffn,
    w_shared_gate,
    w_shared_up,
    w_shared_down,
    expert_gate_weight,
    expert_up_weight,
    expert_down_weight,
    cotangent,
):
    own, width = tokens.shape
    cols = lax.axis_size("col")
    col = lax.axis_index("col")
    devices = lax.axis_size("row") * cols
    group = own * cols
    ring = Ring()
    order = jnp.asarray(col_order(), jnp.int32) ^ col
    steps = jnp.arange(own, dtype=jnp.int32)
    where = (order[:, None] * own + steps[None, :]).reshape(group)

    rows_n, topk = (ring.n, routed_expert_index.shape[1])

    shard, small = w_latent.shape[0], gain_latent.shape[0]
    lat_lanes = -(-(DC + DR) // 128) * 128
    packed = jnp.stack(
        [
            jnp.pad(gain_latent, (0, shard - small)),
            gain_attn,
            gain_ffn,
        ]
    )
    packed = jnp.concatenate(
        [
            jnp.pad(w_latent, ((0, 0), (0, lat_lanes - DC - DR))),
            jnp.pad(packed, ((0, shard - 3), (0, 128 - shard))),
        ],
        axis=1,
    )
    packed = col_gather(packed)
    listed = col_order()
    packed = [packed[j * shard : (j + 1) * shard] for j in range(cols)]
    packed = jnp.concatenate(col_flip([packed[listed.index(k)] for k in range(cols)]), axis=0)
    high = lax.reduce_precision(routed_gate_weight, 8, 7)
    middle = lax.reduce_precision(routed_gate_weight - high, 8, 7)
    low = routed_gate_weight - high - middle
    info = jnp.concatenate([routed_expert_index.astype(F32), high, middle, low], axis=1)
    info = info.astype(BF16)
    count = packed.shape[0]
    tall = -(-own // count)
    info = info.reshape(tall, own // tall, 4 * topk).transpose(1, 0, 2).reshape(own // tall, -1)
    info_at = lat_lanes + shard
    info_wide = info.shape[1]
    lanes = -(-(info_at + info_wide) // 128) * 128
    packed = jnp.pad(packed, ((0, 0), (0, lanes - packed.shape[1])))
    packed = packed + jnp.pad(
        info, ((0, count - own // tall), (info_at, lanes - info_at - info_wide))
    )
    dgathered = ring.gather(cotangent)
    for block in dgathered[-3:-1]:
        packed = after(packed, block[0, 0])
    packed = ring.gather(packed)
    first = packed[-1][0, 0]
    packed = lax.optimization_barrier(jnp.concatenate(packed, axis=0))
    wlat = packed[:, : DC + DR]
    gains = packed.reshape(rows_n, cols, shard, lanes)[:, :, :3, lat_lanes : lat_lanes + shard]
    gains = gains.astype(F32)
    g_attn = gains[:, :, 1].reshape(width)
    g_ffn = gains[:, :, 2].reshape(width)
    g_lat = ring.absolute(gains[:, :, 0, :small].reshape(rows_n, cols * small), 0).reshape(-1)
    info = packed.reshape(rows_n, count, lanes)[:, : own // tall, info_at : info_at + info_wide]
    info = info.reshape(rows_n, own // tall, tall, 4 * topk).transpose(0, 2, 1, 3)
    info = info.reshape(rows_n * own, 4 * topk)
    routes = Routes(info, own, topk, cols, rows_n, 2 * E // devices)

    blk = w_query.shape[0]
    wq_n, wkv_n, wo_n = (w_query.shape[1], w_kv_up.size // blk, w_out.shape[0])
    lat_blk = w_kv_up.shape[0]
    fold = blk // lat_blk
    mixed = w_kv_up.reshape(lat_blk, fold, wkv_n).transpose(1, 0, 2).reshape(blk, wkv_n)
    mixed = jnp.concatenate([w_query, mixed, w_out.T], axis=1)
    attention = ring.gather(after(mixed, first))
    last = attention[-1][0, 0]
    attention = jnp.concatenate(attention, axis=0)
    wq = attention[:, :wq_n]
    wo = attention[:, wq_n + wkv_n :]
    wkv = attention[:, wq_n : wq_n + wkv_n].reshape(rows_n, fold, lat_blk, wkv_n)
    wkv = wkv.transpose(0, 2, 1, 3).reshape(DC, fold * wkv_n)

    dexp = dot(routes.chosen, jnp.concatenate(dgathered, axis=0), 1, 0) * routes.gate_of_row

    rows = jnp.concatenate(ring.relative(tokens, 1), axis=1).astype(F32)
    grad_low = jnp.concatenate(ring.relative(cotangent, 1), axis=1)
    grad_own = grad_low.astype(F32)
    factor_one = inv_rms(rows)
    xhat = rows * factor_one
    grad_grp = col_gather(grad_low)
    ready = after(after(jnp.float32(1.0), grad_grp[-1, -1]), dgathered[-1][0, 0])
    xn = (xhat * ready * g_attn).astype(BF16)
    segment, position = seq_layout(seq_lengths[0], where)
    cosine, sine = rope_tables(position, DR)
    cos_own, sin_own = (cosine[:own], sine[:own])
    latent_pre = dot(xn, wlat, 1, 0)
    pre_lat = latent_pre[:, :DC]
    factor_lat = inv_rms(pre_lat)
    lat_hat = pre_lat * factor_lat
    ckv_own = jnp.concatenate(
        [
            (lat_hat * g_lat).astype(BF16),
            rotate(latent_pre[:, DC:], cos_own, sin_own).astype(BF16),
        ],
        axis=1,
    )
    xn_grp, ckv_grp = (col_gather(xn), col_gather(ckv_own))
    dreceived = routes.send(after(dexp, xn_grp[-1, -1]).astype(BF16))
    heads = wq.shape[1] // (DN + DR)
    query = dot(xn_grp, wq, 1, 0).reshape(group, heads, DN + DR)
    query = jnp.concatenate(
        [query[..., :DN], rotate(query[..., DN:], cosine[:, None, :], sine[:, None, :])], axis=-1
    ).astype(BF16)
    to_ring = ring.order_matrix(DC)
    latent_grp = dot(ckv_grp[:, :DC], to_ring, 1, 0).astype(BF16)
    pairs = dot(latent_grp, wkv, 1, 0).astype(BF16).reshape(group, heads, DN + DV)
    keys = jnp.concatenate(
        [pairs[..., :DN], jnp.broadcast_to(ckv_grp[:, None, DC:], (group, heads, DR))], axis=-1
    )
    values = pairs[..., DN:]
    scale = after(jnp.float32(1.0 / math.sqrt(DN + DR)), dexp[0, 0])
    mask = (segment[:, None] == segment[None, :]) & (where[None, :] <= where[:, None])
    raw = jnp.einsum("qhd,khd->hqk", query, keys, preferred_element_type=F32) * scale
    scores = jnp.where(mask[None], raw, NEG)
    top = jnp.max(scores, axis=-1, keepdims=True)
    lse = top + jnp.log(jnp.sum(jnp.exp(scores - top), axis=-1, keepdims=True))
    prob = jnp.where(mask[None], jnp.exp(scores - lse), 0.0)
    prob_low = prob.astype(BF16)
    attended = (
        jnp.einsum("hqk,khd->qhd", prob_low, values, preferred_element_type=F32)
        .astype(BF16)
        .reshape(group, heads * DV)
    )
    hidden = rows + col_scatter(dot(attended, wo, 1, 1))
    factor_two = inv_rms(hidden)
    hhat = hidden * factor_two
    h2n = (hhat * g_ffn).astype(BF16)

    gathered = ring.gather(ring.absolute(h2n, 1))
    h2n_grp = col_gather(h2n)
    arrived = dot(routes.chosen, jnp.concatenate(gathered, axis=0), 1, 0)
    arrived = routes.send(after(arrived, h2n_grp[-1, -1]).astype(BF16))
    units = arrived.shape[0]
    shape = expert_gate_weight.shape
    wg, wu, wd = (
        w.reshape(units, -1, width)
        for w in (expert_gate_weight, expert_up_weight, expert_down_weight)
    )
    pre_gate = jnp.einsum("urd,uhd->urh", arrived, wg, preferred_element_type=F32)
    pre_up = jnp.einsum("urd,uhd->urh", arrived, wu, preferred_element_type=F32)
    dact = jnp.einsum("urd,uhd->urh", dreceived, wd, preferred_element_type=F32)
    act, slope = swish_parts(pre_gate)
    exp_hidden = (act * pre_up).astype(BF16)
    dgate = (dact * pre_up * slope).astype(BF16)
    dup = (dact * act).astype(BF16)
    dx_exp = (
        jnp.einsum("urh,uhd->urd", dgate, wg, preferred_element_type=F32)
        + jnp.einsum("urh,uhd->urd", dup, wu, preferred_element_type=F32)
    ).astype(BF16)
    dx_back = routes.give_back(dx_exp)
    exp_hidden = after(exp_hidden, dx_exp[0, 0, 0])
    exp_out = jnp.einsum("urh,uhd->urd", exp_hidden, wd, preferred_element_type=F32).astype(BF16)

    ffs = w_shared_gate.shape[1]
    shared = jnp.concatenate([w_shared_gate, w_shared_up, w_shared_down.T], axis=1)
    shared = jnp.concatenate(ring.gather(after(shared, last)), axis=0)
    wsgu, wsd = (shared[:, : 2 * ffs], shared[:, 2 * ffs :])
    pre_both = dot(h2n_grp, wsgu, 1, 0)
    pre_gate, pre_up = (pre_both[:, :ffs], pre_both[:, ffs:])
    act_shared, slope_shared = swish_parts(pre_gate)
    shared_act = (act_shared * pre_up).astype(BF16)
    shared_own = col_scatter(dot(shared_act, wsd, 1, 1))
    dshared = dot(grad_grp, wsd, 1, 0)
    dboth = jnp.concatenate(
        [
            (dshared * pre_up * slope_shared).astype(BF16),
            (dshared * act_shared).astype(BF16),
        ],
        axis=1,
    )
    terms = col_scatter(dot(dboth, wsgu, 1, 1))
    g_shared = jnp.concatenate(
        [dot(h2n_grp, dboth, 0, 0).astype(BF16), dot(grad_grp, shared_act, 0, 0).astype(BF16)],
        axis=1,
    )
    shared_terms = ring.cut(g_shared, 0)
    arrived, dreceived = (after(arrived, dx_exp[0, 0, 0]), after(dreceived, dx_exp[0, 0, 0]))
    expert_down_gradient = jnp.einsum(
        "urh,urd->uhd", exp_hidden, dreceived, preferred_element_type=F32
    ).reshape(shape)
    expert_gate_gradient = jnp.einsum(
        "urh,urd->uhd", dgate, arrived, preferred_element_type=F32
    ).reshape(shape)
    expert_up_gradient = jnp.einsum(
        "urh,urd->uhd", dup, arrived, preferred_element_type=F32
    ).reshape(shape)

    dmoe = after(dot(routes.chosen, dx_back, 0, 0), exp_out[0, 0, 0]).astype(BF16)
    dmoe = ring.scatter(ring.cut(dmoe, 0))
    g_shared = ring.scatter(shared_terms)
    g_shared_gate, g_shared_up = (g_shared[:, :ffs], g_shared[:, ffs : 2 * ffs])
    g_shared_down = g_shared[:, 2 * ffs :].T
    dmoe = jnp.concatenate(ring.relative(dmoe, 1), axis=1)
    dh2n = terms + dmoe
    ffn_gain_gradient = jnp.sum(dh2n * hhat, axis=0)
    dhidden = grad_own + norm_gradient_pass(dh2n, hhat, factor_two, g_ffn)
    dattn = col_gather(dhidden.astype(BF16))
    out_back = routes.give_back(after(exp_out, dattn[-1, -1]))
    moe = ring.scatter(ring.cut(dot(routes.gates, out_back, 0, 0).astype(BF16), 0))
    g_out = dot(dattn, attended, 0, 0).astype(BF16)
    dattended = dot(dattn, wo, 1, 0).astype(BF16).reshape(group, heads, DV)

    dprob = jnp.einsum("qhd,khd->hqk", dattended, values, preferred_element_type=F32)
    delta = jnp.sum(prob * dprob, axis=-1, keepdims=True)
    dscore = (prob * (dprob - delta) * scale).astype(BF16)
    dquery = jnp.einsum("hqk,khd->qhd", dscore, keys, preferred_element_type=F32)
    dkeys = jnp.einsum("hqk,qhd->khd", dscore, query, preferred_element_type=F32)
    dvalues = jnp.einsum("hqk,qhd->khd", prob_low, dattended, preferred_element_type=F32)
    dquery_pre = jnp.concatenate(
        [dquery[..., :DN], unrotate(dquery[..., DN:], cosine[:, None, :], sine[:, None, :])],
        axis=-1,
    )
    dquery_pre = dquery_pre.reshape(group, heads * (DN + DR)).astype(BF16)
    dpairs = (
        jnp.concatenate([dkeys[..., :DN], dvalues], axis=-1)
        .reshape(group, heads * (DN + DV))
        .astype(BF16)
    )
    dkey_rope = jnp.sum(dkeys[..., DN:], axis=1)
    dckv = col_scatter(jnp.concatenate([dot(dpairs, wkv, 1, 1), dkey_rope], axis=1))
    dxn = col_scatter(dot(dquery_pre, wq, 1, 1))
    g_query = dot(xn_grp, dquery_pre, 0, 0).astype(BF16)
    g_kv = dot(latent_grp, dpairs, 0, 0).astype(BF16).reshape(rows_n, lat_blk, fold, wkv_n)
    g_kv = g_kv.transpose(0, 2, 1, 3).reshape(rows_n * blk, wkv_n)
    g_attention = ring.scatter(ring.cut(jnp.concatenate([g_query, g_kv, g_out], axis=1), 0))
    g_query = g_attention[:, :wq_n]
    g_kv = g_attention[:, wq_n : wq_n + wkv_n].reshape(fold, lat_blk, wkv_n)
    g_kv = g_kv.transpose(1, 0, 2).reshape(w_kv_up.shape)
    g_out = g_attention[:, wq_n + wkv_n :].T

    dlatent = lax.dot_general(
        dckv[:, :DC],
        to_ring.astype(F32),
        (((1,), (1,)), ((), ())),
        precision=lax.Precision.HIGHEST,
        preferred_element_type=F32,
    )
    latent_gain_gradient = jnp.sum(dlatent * lat_hat, axis=0)
    dlatent_pre = jnp.concatenate(
        [
            norm_gradient_pass(dlatent, lat_hat, factor_lat, g_lat),
            unrotate(dckv[:, DC:], cos_own, sin_own),
        ],
        axis=1,
    ).astype(BF16)
    dxnorm = dxn + dot(dlatent_pre, wlat, 1, 1)
    attn_gain_gradient = jnp.sum(dxnorm * xhat, axis=0)
    input_gradient = dhidden + norm_gradient_pass(dxnorm, xhat, factor_one, g_attn)
    input_gradient = ring.absolute(input_gradient.astype(BF16), 1)
    layer_output = ring.absolute(hidden + shared_own, 1) + moe
    layer_output = layer_output.astype(BF16)

    small_terms = jnp.concatenate(ring.relative(latent_gain_gradient.reshape(rows_n, -1), 0), axis=0)
    small_terms = small_terms.reshape(rows_n * cols, 1, small)
    small_terms = jnp.concatenate(
        [
            jnp.pad(small_terms, ((0, 0), (0, 0), (0, shard - small))),
            attn_gain_gradient.reshape(rows_n * cols, 1, shard),
            ffn_gain_gradient.reshape(rows_n * cols, 1, shard),
        ],
        axis=1,
    )
    small_terms = jnp.pad(small_terms, ((0, 0), (0, shard - 3), (0, 128 - shard)))
    latent_terms = jnp.concatenate(
        [
            dot(xn, jnp.pad(dlatent_pre, ((0, 0), (0, lat_lanes - DC - DR))), 0, 0),
            small_terms.reshape(width, 128),
        ],
        axis=1,
    )
    latent_terms = ring.scatter(ring.cut(latent_terms, 0))
    latent_terms = col_flip([latent_terms[k * shard : (k + 1) * shard] for k in range(cols)])
    latent_terms = jnp.concatenate([latent_terms[k] for k in listed], axis=0)
    latent_terms = col_scatter(latent_terms)
    return (
        layer_output,
        input_gradient,
        latent_terms[1, lat_lanes : lat_lanes + shard],
        g_query,
        latent_terms[:, : DC + DR],
        latent_terms[0, lat_lanes : lat_lanes + small],
        g_kv,
        g_out,
        latent_terms[2, lat_lanes : lat_lanes + shard],
        g_shared_gate,
        g_shared_up,
        g_shared_down,
        expert_gate_gradient,
        expert_up_gradient,
        expert_down_gradient,
    )


def solution(mesh):
    return jax.shard_map(
        on_device,
        mesh=mesh,
        in_specs=(
            P(("row", "col"), None),
            P("row", None),
            P(("row", "col"), None),
            P(("row", "col"), None),
            P(("row", "col")),
            P("row", "col"),
            P(("row", "col"), None),
            P(("row", "col")),
            P("row", "col"),
            P("col", "row"),
            P(("row", "col")),
            P("row", "col"),
            P("row", "col"),
            P("col", "row"),
            P(("row", "col"), None, None),
            P(("row", "col"), None, None),
            P(("row", "col"), None, None),
            P(("row", "col"), None),
        ),
        out_specs=(
            P(("row", "col"), None),
            P(("row", "col"), None),
            P(("row", "col")),
            P("row", "col"),
            P(("row", "col"), None),
            P(("row", "col")),
            P("row", "col"),
            P("col", "row"),
            P(("row", "col")),
            P("row", "col"),
            P("row", "col"),
            P("col", "row"),
            P(("row", "col"), None, None),
            P(("row", "col"), None, None),
            P(("row", "col"), None, None),
        ),
        check_vma=False,
    )
```

```python
import math

import jax
import jax.numpy as jnp
from jax import lax
from jax.sharding import PartitionSpec as P

DN = 128
DR = 64
DV = 128
DC = 512
E = 64
CAP = 18


EPS = 1e-06
NEG = -1e30
F32 = jnp.float32
BF16 = jnp.bfloat16


def inv_rms(rows):
    return lax.rsqrt(jnp.mean(rows * rows, axis=-1, keepdims=True) + EPS)


def norm_gradient_pass(grad_out, normed, factor, gain):
    scaled = grad_out * gain
    return factor * (scaled - normed * jnp.mean(scaled * normed, axis=-1, keepdims=True))


def swish_parts(pre):
    sig = jax.nn.sigmoid(pre)
    return (pre * sig, sig * (1.0 + pre * (1.0 - sig)))


def rope_tables(position, width):
    half = width // 2
    freq = jnp.exp(jnp.arange(half, dtype=F32) * (-2.0 * math.log(10000.0) / width))
    angle = freq[:, None] * position.astype(F32)[None, :]
    return (jnp.cos(angle).T, jnp.sin(angle).T)


def rotate(values, cosine, sine):
    half = values.shape[-1] // 2
    first, second = (values[..., :half], values[..., half:])
    return jnp.concatenate(
        [first * cosine - second * sine, first * sine + second * cosine], axis=-1
    )


def unrotate(grads, cosine, sine):
    half = grads.shape[-1] // 2
    first, second = (grads[..., :half], grads[..., half:])
    return jnp.concatenate(
        [first * cosine + second * sine, second * cosine - first * sine], axis=-1
    )


def seq_layout(lengths, where):
    ends = jnp.cumsum(lengths)
    after = where[:, None] >= ends[None, :]
    segment = jnp.sum(after.astype(jnp.int32), axis=1)
    begin = jnp.sum(jnp.where(after, lengths[None, :], 0), axis=1)
    return (segment, where - begin)


def dot(a, b, ca, cb):
    return lax.dot_general(a, b, (((ca,), (cb,)), ((), ())), preferred_element_type=F32)


def col_bits():
    bit, bits = lax.axis_size("col") // 2, []
    while bit:
        bits.append(bit)
        bit //= 2
    return bits


def col_order():
    order = [0]
    for bit in col_bits():
        order = order + [one ^ bit for one in order]
    return order


def col_flip(blocks):
    col = lax.axis_index("col")
    for bit in col_bits():
        on = (col & bit) != 0
        blocks = [jnp.where(on, blocks[k ^ bit], blocks[k]) for k in range(len(blocks))]
    return blocks


def col_swap(block, bit):
    return lax.ppermute(block, "col", [(i, i ^ bit) for i in range(lax.axis_size("col"))])


def col_gather(block):
    for bit in col_bits():
        block = jnp.concatenate([block, col_swap(block, bit)], axis=0)
    return block


def col_scatter(terms):
    for bit in reversed(col_bits()):
        half = terms.shape[0] // 2
        terms = terms[:half] + col_swap(terms[half:].astype(BF16), bit).astype(F32)
    return terms


class Ring:
    def __init__(self):
        n = lax.axis_size("row")
        self.n = n
        ring = list(range(0, n, 2)) + list(range(1, n, 2))[::-1]
        spot = [ring.index(i) for i in range(n)]
        self.ahead = [(ring[i], ring[(i + 1) % n]) for i in range(n)]
        self.behind = [(b, a) for a, b in self.ahead]
        self.most = n // 2
        offsets = [0]
        for step in range(1, self.most + 1):
            offsets.append(-step)
            if step < n - self.most:
                offsets.append(step)
        self.block_of = {off % n: j for j, off in enumerate(offsets)}
        self.ring, self.spot = ring, spot
        self.turns = [off % n for off in offsets]
        index = lax.axis_index("row")
        half = lax.shift_right_logical(index, 1)
        self.me = jnp.where((index & 1) == 0, half, n - 1 - half)

    def gather(self, block):
        a = b = block
        out = [block]
        for step in range(1, self.most + 1):
            a = lax.ppermute(a, "row", self.ahead)
            out.append(a)
            if step < self.n - self.most:
                b = lax.ppermute(b, "row", self.behind)
                out.append(b)
        return out

    def scatter(self, blocks):
        def pick(off):
            return blocks[self.block_of[off % self.n]]

        total = blocks[0]
        if self.n == 1:
            return total
        a = pick(self.most)
        for step in range(self.most - 1, 0, -1):
            a = lax.ppermute(a.astype(BF16), "row", self.ahead).astype(F32) + pick(step)
        total = total + lax.ppermute(a.astype(BF16), "row", self.ahead).astype(F32)
        most = self.n - 1 - self.most
        if most:
            b = pick(-most)
            for step in range(most - 1, 0, -1):
                b = lax.ppermute(b.astype(BF16), "row", self.behind).astype(F32) + pick(-step)
            total = total + lax.ppermute(b.astype(BF16), "row", self.behind).astype(F32)
        return total

    def turn(self, blocks, start, axis):
        size = blocks[0].shape[axis]
        twice = jnp.concatenate(blocks + blocks, axis=axis)
        at = [0] * twice.ndim
        at[axis] = start * size
        shape = list(twice.shape)
        shape[axis] = self.n * size
        turned = lax.dynamic_slice(twice, at, shape, allow_negative_indices=False)
        return self.cut(turned, axis)

    def relative(self, values, axis):
        blocks = self.cut(values, axis)
        blocks = self.turn([blocks[k] for k in self.ring], self.me, axis)
        return [blocks[turn] for turn in self.turns]

    def absolute(self, values, axis):
        blocks = self.cut(values, axis)
        blocks = [blocks[self.block_of[i]] for i in range(self.n)]
        blocks = self.turn(blocks, self.n - self.me, axis)
        return jnp.concatenate([blocks[self.spot[k]] for k in range(self.n)], axis=axis)

    def order_matrix(self, count):
        size = count // self.n
        steps = jnp.arange(count, dtype=jnp.int32)
        turns = jnp.asarray([t for t in self.turns for _ in range(size)], jnp.int32)
        place = self.me + turns
        place = jnp.where(place >= self.n, place - self.n, place)
        owner = jnp.where(2 * place < self.n, 2 * place, 2 * (self.n - 1 - place) + 1)
        wanted = owner * size + steps % size
        return (wanted[None, :] == steps[:, None]).astype(BF16)

    def cut(self, values, axis):
        size = values.shape[axis] // self.n
        return [lax.slice_in_dim(values, j * size, (j + 1) * size, axis=axis) for j in range(self.n)]


def after(value, earlier):
    return value + jnp.where(jnp.isfinite(earlier.astype(F32)), 0.0, 1.0).astype(value.dtype)


class Routes:
    def __init__(self, info, own, topk, cols, rows, per):
        self.joined = per % 2 == 0
        self.units = per // 2 if self.joined else per
        self.cols = cols
        self.places = cols if self.joined else cols // 2
        self.span = rows * CAP
        mine = self.places * self.units
        listed = info.T.astype(F32)
        names = listed[:topk].astype(jnp.int32)
        weights = listed[topk : 2 * topk] + listed[2 * topk : 3 * topk]
        weights = weights + listed[3 * topk : 4 * topk]
        first = lax.axis_index("row") * mine
        experts = first + jnp.arange(mine, dtype=jnp.int32)
        hits = names[None] == experts[:, None, None]
        named = jnp.any(hits, axis=1)
        gates = jnp.sum(jnp.where(hits, weights[None], 0.0), axis=1)
        steps = jnp.arange(own, dtype=jnp.int32)
        earlier = (steps[:, None] < steps[None, :]).astype(BF16)
        before = dot(named.astype(BF16).reshape(mine * rows, own), earlier, 1, 0)
        before = before.astype(jnp.int32).reshape(mine, rows, own)
        before = before + (jnp.arange(rows, dtype=jnp.int32) * CAP)[None, :, None]
        slot = jnp.where(named, before.reshape(mine, rows * own), -1)
        spot = jnp.arange(self.span, dtype=jnp.int32)
        chosen = slot[:, None, :] == spot[None, :, None]
        weighed = jnp.where(chosen, gates[:, None, :], 0.0)
        shape = (mine * self.span, rows * own)
        self.chosen = chosen.astype(BF16).reshape(shape)
        self.gate_of_row = jnp.sum(weighed, axis=2).reshape(shape[0], 1)
        self.gates = weighed.astype(BF16).reshape(shape)

    def send(self, rows):
        width = rows.shape[1]
        parts = rows.reshape(self.places, self.units * self.span, width)
        if not self.joined:
            parts = jnp.broadcast_to(parts[:, None], (self.places, 2) + parts.shape[1:])
            parts = parts.reshape(self.cols, self.units * self.span, width)
        got = lax.all_to_all(parts, "col", split_axis=0, concat_axis=0, tiled=True)
        got = got.reshape(self.cols, self.units, self.span, width)
        return got.transpose(1, 0, 2, 3).reshape(self.units, self.cols * self.span, width)

    def give_back(self, results):
        width = results.shape[-1]
        parts = results.reshape(self.units, self.cols, self.span, width).transpose(1, 0, 2, 3)
        parts = parts.reshape(self.cols, self.units * self.span, width)
        got = lax.all_to_all(parts, "col", split_axis=0, concat_axis=0, tiled=True)
        if not self.joined:
            got = got.reshape((self.places, 2) + got.shape[1:]).astype(F32)
            got = jnp.sum(got, axis=1).astype(BF16)
        return got.reshape(self.places * self.units * self.span, width)


def on_device(
    tokens,
    seq_lengths,
    routed_expert_index,
    routed_gate_weight,
    gain_attn,
    w_query,
    w_latent,
    gain_latent,
    w_kv_up,
    w_out,
    gain_ffn,
    w_shared_gate,
    w_shared_up,
    w_shared_down,
    expert_gate_weight,
    expert_up_weight,
    expert_down_weight,
    cotangent,
):
    own, width = tokens.shape
    cols = lax.axis_size("col")
    col = lax.axis_index("col")
    devices = lax.axis_size("row") * cols
    group = own * cols
    ring = Ring()
    order = jnp.asarray(col_order(), jnp.int32) ^ col
    steps = jnp.arange(own, dtype=jnp.int32)
    where = (order[:, None] * own + steps[None, :]).reshape(group)

    rows_n, topk = (ring.n, routed_expert_index.shape[1])

    shard, small = w_latent.shape[0], gain_latent.shape[0]
    lat_lanes = -(-(DC + DR) // 128) * 128
    packed = jnp.stack(
        [
            jnp.pad(gain_latent, (0, shard - small)),
            gain_attn,
            gain_ffn,
        ]
    )
    packed = jnp.concatenate(
        [
            jnp.pad(w_latent, ((0, 0), (0, lat_lanes - DC - DR))),
            jnp.pad(packed, ((0, shard - 3), (0, 128 - shard))),
        ],
        axis=1,
    )
    packed = col_gather(packed)
    listed = col_order()
    packed = [packed[j * shard : (j + 1) * shard] for j in range(cols)]
    packed = jnp.concatenate(col_flip([packed[listed.index(k)] for k in range(cols)]), axis=0)
    high = lax.reduce_precision(routed_gate_weight, 8, 7)
    middle = lax.reduce_precision(routed_gate_weight - high, 8, 7)
    low = routed_gate_weight - high - middle
    info = jnp.concatenate([routed_expert_index.astype(F32), high, middle, low], axis=1)
    info = info.astype(BF16)
    count = packed.shape[0]
    tall = -(-own // count)
    info = info.reshape(tall, own // tall, 4 * topk).transpose(1, 0, 2).reshape(own // tall, -1)
    info_at = lat_lanes + shard
    info_wide = info.shape[1]
    lanes = -(-(info_at + info_wide) // 128) * 128
    packed = jnp.pad(packed, ((0, 0), (0, lanes - packed.shape[1])))
    packed = packed + jnp.pad(
        info, ((0, count - own // tall), (info_at, lanes - info_at - info_wide))
    )
    dgathered = ring.gather(cotangent)
    for block in dgathered[-3:-1]:
        packed = after(packed, block[0, 0])
    packed = ring.gather(packed)
    first = packed[-1][0, 0]
    packed = lax.optimization_barrier(jnp.concatenate(packed, axis=0))
    wlat = packed[:, : DC + DR]
    gains = packed.reshape(rows_n, cols, shard, lanes)[:, :, :3, lat_lanes : lat_lanes + shard]
    gains = gains.astype(F32)
    g_attn = gains[:, :, 1].reshape(width)
    g_ffn = gains[:, :, 2].reshape(width)
    g_lat = ring.absolute(gains[:, :, 0, :small].reshape(rows_n, cols * small), 0).reshape(-1)
    info = packed.reshape(rows_n, count, lanes)[:, : own // tall, info_at : info_at + info_wide]
    info = info.reshape(rows_n, own // tall, tall, 4 * topk).transpose(0, 2, 1, 3)
    info = info.reshape(rows_n * own, 4 * topk)
    routes = Routes(info, own, topk, cols, rows_n, 2 * E // devices)

    blk = w_query.shape[0]
    wq_n, wkv_n, wo_n = (w_query.shape[1], w_kv_up.size // blk, w_out.shape[0])
    lat_blk = w_kv_up.shape[0]
    fold = blk // lat_blk
    mixed = w_kv_up.reshape(lat_blk, fold, wkv_n).transpose(1, 0, 2).reshape(blk, wkv_n)
    mixed = jnp.concatenate([w_query, mixed, w_out.T], axis=1)
    attention = ring.gather(after(mixed, first))
    last = attention[-1][0, 0]
    attention = jnp.concatenate(attention, axis=0)
    wq = attention[:, :wq_n]
    wo = attention[:, wq_n + wkv_n :]
    wkv = attention[:, wq_n : wq_n + wkv_n].reshape(rows_n, fold, lat_blk, wkv_n)
    wkv = wkv.transpose(0, 2, 1, 3).reshape(DC, fold * wkv_n)

    dexp = dot(routes.chosen, jnp.concatenate(dgathered, axis=0), 1, 0) * routes.gate_of_row

    both = jnp.concatenate([tokens, cotangent], axis=0)
    both = dot(both, ring.order_matrix(width), 1, 0)
    rows = both[:own]
    grad_low = both[own:].astype(BF16)
    grad_own = grad_low.astype(F32)
    factor_one = inv_rms(rows)
    xhat = rows * factor_one
    grad_grp = col_gather(grad_low)
    ready = after(after(jnp.float32(1.0), grad_grp[-1, -1]), dgathered[-1][0, 0])
    xn = (xhat * ready * g_attn).astype(BF16)
    segment, position = seq_layout(seq_lengths[0], where)
    cosine, sine = rope_tables(position, DR)
    cos_own, sin_own = (cosine[:own], sine[:own])
    latent_pre = dot(xn, wlat, 1, 0)
    pre_lat = latent_pre[:, :DC]
    factor_lat = inv_rms(pre_lat)
    lat_hat = pre_lat * factor_lat
    ckv_own = jnp.concatenate(
        [
            (lat_hat * g_lat).astype(BF16),
            rotate(latent_pre[:, DC:], cos_own, sin_own).astype(BF16),
        ],
        axis=1,
    )
    xn_grp, ckv_grp = (col_gather(xn), col_gather(ckv_own))
    heads = wq.shape[1] // (DN + DR)
    query = dot(xn_grp, wq, 1, 0).reshape(group, heads, DN + DR)
    query = jnp.concatenate(
        [query[..., :DN], rotate(query[..., DN:], cosine[:, None, :], sine[:, None, :])], axis=-1
    ).astype(BF16)
    to_ring = ring.order_matrix(DC)
    latent_grp = dot(ckv_grp[:, :DC], to_ring, 1, 0).astype(BF16)
    pairs = dot(latent_grp, wkv, 1, 0).astype(BF16).reshape(group, heads, DN + DV)
    keys = jnp.concatenate(
        [pairs[..., :DN], jnp.broadcast_to(ckv_grp[:, None, DC:], (group, heads, DR))], axis=-1
    )
    values = pairs[..., DN:]
    shared = jnp.concatenate([w_shared_gate, w_shared_up, w_shared_down.T], axis=1)
    shared = ring.gather(after(shared, last))
    scale = after(jnp.float32(1.0 / math.sqrt(DN + DR)), shared[1][0, 0])
    mask = (segment[:, None] == segment[None, :]) & (where[None, :] <= where[:, None])
    raw = jnp.einsum("qhd,khd->hqk", query, keys, preferred_element_type=F32) * scale
    scores = jnp.where(mask[None], raw, NEG)
    top = jnp.max(scores, axis=-1, keepdims=True)
    lse = top + jnp.log(jnp.sum(jnp.exp(scores - top), axis=-1, keepdims=True))
    prob = jnp.where(mask[None], jnp.exp(scores - lse), 0.0)
    prob_low = prob.astype(BF16)
    attended = (
        jnp.einsum("hqk,khd->qhd", prob_low, values, preferred_element_type=F32)
        .astype(BF16)
        .reshape(group, heads * DV)
    )
    hidden = rows + col_scatter(dot(attended, wo, 1, 1))
    dreceived = routes.send(after(dexp, hidden[0, 0]).astype(BF16))
    factor_two = inv_rms(hidden)
    hhat = hidden * factor_two
    h2n = (hhat * g_ffn).astype(BF16)

    gathered = ring.gather(ring.absolute(h2n, 1))
    h2n_grp = col_gather(h2n)
    arrived = dot(routes.chosen, jnp.concatenate(gathered, axis=0), 1, 0)
    arrived = routes.send(after(arrived, h2n_grp[-1, -1]).astype(BF16))
    units = arrived.shape[0]
    shape = expert_gate_weight.shape
    wg, wu, wd = (
        w.reshape(units, -1, width)
        for w in (expert_gate_weight, expert_up_weight, expert_down_weight)
    )
    pre_gate = jnp.einsum("urd,uhd->urh", arrived, wg, preferred_element_type=F32)
    pre_up = jnp.einsum("urd,uhd->urh", arrived, wu, preferred_element_type=F32)
    dact = jnp.einsum("urd,uhd->urh", dreceived, wd, preferred_element_type=F32)
    act, slope = swish_parts(pre_gate)
    exp_hidden = (act * pre_up).astype(BF16)
    dgate = (dact * pre_up * slope).astype(BF16)
    dup = (dact * act).astype(BF16)
    dx_exp = (
        jnp.einsum("urh,uhd->urd", dgate, wg, preferred_element_type=F32)
        + jnp.einsum("urh,uhd->urd", dup, wu, preferred_element_type=F32)
    ).astype(BF16)
    dx_back = routes.give_back(dx_exp)
    exp_hidden = after(exp_hidden, dx_exp[0, 0, 0])
    exp_out = jnp.einsum("urh,uhd->urd", exp_hidden, wd, preferred_element_type=F32).astype(BF16)

    ffs = w_shared_gate.shape[1]
    shared = jnp.concatenate(shared, axis=0)
    wsgu, wsd = (shared[:, : 2 * ffs], shared[:, 2 * ffs :])
    pre_both = dot(h2n_grp, wsgu, 1, 0)
    pre_gate, pre_up = (pre_both[:, :ffs], pre_both[:, ffs:])
    act_shared, slope_shared = swish_parts(pre_gate)
    shared_act = (act_shared * pre_up).astype(BF16)
    shared_own = col_scatter(dot(shared_act, wsd, 1, 1))
    dshared = dot(grad_grp, wsd, 1, 0)
    dboth = jnp.concatenate(
        [
            (dshared * pre_up * slope_shared).astype(BF16),
            (dshared * act_shared).astype(BF16),
        ],
        axis=1,
    )
    terms = col_scatter(dot(dboth, wsgu, 1, 1))
    g_shared = jnp.concatenate(
        [dot(h2n_grp, dboth, 0, 0).astype(BF16), dot(grad_grp, shared_act, 0, 0).astype(BF16)],
        axis=1,
    )
    shared_terms = ring.cut(g_shared, 0)
    arrived, dreceived = (after(arrived, dx_exp[0, 0, 0]), after(dreceived, dx_exp[0, 0, 0]))
    expert_down_gradient = jnp.einsum(
        "urh,urd->uhd", exp_hidden, dreceived, preferred_element_type=F32
    ).reshape(shape)
    expert_gate_gradient = jnp.einsum(
        "urh,urd->uhd", dgate, arrived, preferred_element_type=F32
    ).reshape(shape)
    expert_up_gradient = jnp.einsum(
        "urh,urd->uhd", dup, arrived, preferred_element_type=F32
    ).reshape(shape)

    dmoe = after(dot(routes.chosen, dx_back, 0, 0), exp_out[0, 0, 0]).astype(BF16)
    dmoe = ring.scatter(ring.cut(dmoe, 0))
    g_shared = ring.scatter(shared_terms)
    g_shared_gate, g_shared_up = (g_shared[:, :ffs], g_shared[:, ffs : 2 * ffs])
    g_shared_down = g_shared[:, 2 * ffs :].T
    dmoe = jnp.concatenate(ring.relative(dmoe, 1), axis=1)
    dh2n = terms + dmoe
    ffn_gain_gradient = jnp.sum(dh2n * hhat, axis=0)
    dhidden = grad_own + norm_gradient_pass(dh2n, hhat, factor_two, g_ffn)
    out_back = routes.give_back(after(exp_out, dx_back[0, 0]))
    dattn = col_gather(after(dhidden.astype(BF16), out_back[0, 0]))
    moe = ring.scatter(ring.cut(dot(routes.gates, out_back, 0, 0).astype(BF16), 0))
    g_out = dot(dattn, attended, 0, 0).astype(BF16)
    dattended = dot(dattn, wo, 1, 0).astype(BF16).reshape(group, heads, DV)

    dprob = jnp.einsum("qhd,khd->hqk", dattended, values, preferred_element_type=F32)
    delta = jnp.sum(prob * dprob, axis=-1, keepdims=True)
    dscore = (prob * (dprob - delta) * scale).astype(BF16)
    dquery = jnp.einsum("hqk,khd->qhd", dscore, keys, preferred_element_type=F32)
    dkeys = jnp.einsum("hqk,qhd->khd", dscore, query, preferred_element_type=F32)
    dvalues = jnp.einsum("hqk,qhd->khd", prob_low, dattended, preferred_element_type=F32)
    dquery_pre = jnp.concatenate(
        [dquery[..., :DN], unrotate(dquery[..., DN:], cosine[:, None, :], sine[:, None, :])],
        axis=-1,
    )
    dquery_pre = dquery_pre.reshape(group, heads * (DN + DR)).astype(BF16)
    dpairs = (
        jnp.concatenate([dkeys[..., :DN], dvalues], axis=-1)
        .reshape(group, heads * (DN + DV))
        .astype(BF16)
    )
    dkey_rope = jnp.sum(dkeys[..., DN:], axis=1)
    dckv = col_scatter(jnp.concatenate([dot(dpairs, wkv, 1, 1), dkey_rope], axis=1))
    dxn = col_scatter(dot(dquery_pre, wq, 1, 1))
    g_query = dot(xn_grp, dquery_pre, 0, 0).astype(BF16)
    g_kv = dot(latent_grp, dpairs, 0, 0).astype(BF16).reshape(rows_n, lat_blk, fold, wkv_n)
    g_kv = g_kv.transpose(0, 2, 1, 3).reshape(rows_n * blk, wkv_n)
    g_attention = ring.scatter(ring.cut(jnp.concatenate([g_query, g_kv, g_out], axis=1), 0))
    g_query = g_attention[:, :wq_n]
    g_kv = g_attention[:, wq_n : wq_n + wkv_n].reshape(fold, lat_blk, wkv_n)
    g_kv = g_kv.transpose(1, 0, 2).reshape(w_kv_up.shape)
    g_out = g_attention[:, wq_n + wkv_n :].T

    dlatent = lax.dot_general(
        dckv[:, :DC],
        to_ring.astype(F32),
        (((1,), (1,)), ((), ())),
        precision=lax.Precision.HIGHEST,
        preferred_element_type=F32,
    )
    latent_gain_gradient = jnp.sum(dlatent * lat_hat, axis=0)
    dlatent_pre = jnp.concatenate(
        [
            norm_gradient_pass(dlatent, lat_hat, factor_lat, g_lat),
            unrotate(dckv[:, DC:], cos_own, sin_own),
        ],
        axis=1,
    ).astype(BF16)
    dxnorm = dxn + dot(dlatent_pre, wlat, 1, 1)
    attn_gain_gradient = jnp.sum(dxnorm * xhat, axis=0)
    input_gradient = dhidden + norm_gradient_pass(dxnorm, xhat, factor_one, g_attn)
    input_gradient = ring.absolute(input_gradient.astype(BF16), 1)
    layer_output = ring.absolute(hidden + shared_own, 1) + moe
    layer_output = layer_output.astype(BF16)

    small_terms = jnp.concatenate(ring.relative(latent_gain_gradient.reshape(rows_n, -1), 0), axis=0)
    small_terms = small_terms.reshape(rows_n * cols, 1, small)
    small_terms = jnp.concatenate(
        [
            jnp.pad(small_terms, ((0, 0), (0, 0), (0, shard - small))),
            attn_gain_gradient.reshape(rows_n * cols, 1, shard),
            ffn_gain_gradient.reshape(rows_n * cols, 1, shard),
        ],
        axis=1,
    )
    small_terms = jnp.pad(small_terms, ((0, 0), (0, shard - 3), (0, 128 - shard)))
    latent_terms = jnp.concatenate(
        [
            dot(xn, jnp.pad(dlatent_pre, ((0, 0), (0, lat_lanes - DC - DR))), 0, 0),
            small_terms.reshape(width, 128),
        ],
        axis=1,
    )
    latent_terms = ring.scatter(ring.cut(latent_terms, 0))
    latent_terms = col_flip([latent_terms[k * shard : (k + 1) * shard] for k in range(cols)])
    latent_terms = jnp.concatenate([latent_terms[k] for k in listed], axis=0)
    latent_terms = col_scatter(latent_terms)
    return (
        layer_output,
        input_gradient,
        latent_terms[1, lat_lanes : lat_lanes + shard],
        g_query,
        latent_terms[:, : DC + DR],
        latent_terms[0, lat_lanes : lat_lanes + small],
        g_kv,
        g_out,
        latent_terms[2, lat_lanes : lat_lanes + shard],
        g_shared_gate,
        g_shared_up,
        g_shared_down,
        expert_gate_gradient,
        expert_up_gradient,
        expert_down_gradient,
    )


def solution(mesh):
    return jax.shard_map(
        on_device,
        mesh=mesh,
        in_specs=(
            P(("row", "col"), None),
            P("row", None),
            P(("row", "col"), None),
            P(("row", "col"), None),
            P(("row", "col")),
            P("row", "col"),
            P(("row", "col"), None),
            P(("row", "col")),
            P("row", "col"),
            P("col", "row"),
            P(("row", "col")),
            P("row", "col"),
            P("row", "col"),
            P("col", "row"),
            P(("row", "col"), None, None),
            P(("row", "col"), None, None),
            P(("row", "col"), None, None),
            P(("row", "col"), None),
        ),
        out_specs=(
            P(("row", "col"), None),
            P(("row", "col"), None),
            P(("row", "col")),
            P("row", "col"),
            P(("row", "col"), None),
            P(("row", "col")),
            P("row", "col"),
            P("col", "row"),
            P(("row", "col")),
            P("row", "col"),
            P("row", "col"),
            P("col", "row"),
            P(("row", "col"), None, None),
            P(("row", "col"), None, None),
            P(("row", "col"), None, None),
        ),
        check_vma=False,
    )
```
